32 devices in a mesh: feeder: 8 (over z, core), tm: 4 (over y, x).
Axes of the slice: x: 2, y: 2, z: 4, core: 2. Of those that a mesh axis runs over, the one named last changes fastest.
Arguments:
- node_load: bfloat16 [128, 64, 24, 512], P('feeder', None, 'tm'), may hold values from -6 to 6
- drive_map: bfloat16 [128, 512, 256], P('feeder'), may hold values from -0.25 to 0.25
- decay_rate: float32 [128, 24, 256], P('feeder', 'tm'), may hold values from 0.45 to 1
- counts: int32 [128], P('feeder'), may hold values from 64 to 256
- out_map: float32 [128, 2, 256], P('feeder'), may hold values from -0.375 to 0.375
- area_of: int32 [128, 1], replicated, may hold values from 0 to 7; in each aligned block of 16 rows (0 to 15, 16 to 31, ...) at most 2 rows name the same one
- head_bus: int32 [128], replicated, may hold values from 0 to 255
- rule_of: int32 [128], replicated, may hold values from 0 to 15
- rule_knots: int32 [16, 8], replicated, may hold values from -3200 to 2400, as said below
- levels: int32 [16, 8], replicated, may hold values from -1000 to 1000
- sensitivity: float32 [8, 2, 256, 256], P('feeder'), may hold values from -0.6 to 0.6
Outputs:
- setpoints: float32 [128, 24, 64], P('feeder', 'tm')
The draws below stay inside these ranges and needn't reach their ends.
Inputs may be any that keep to these rules, and one draw needn't show every extreme that they name: `area_of`: in each aligned block of 16 feeders no area is named by more than 2 feeders, a bound that some block reaches. `rule_knots`: each row strictly increasing, neighbouring breakpoints 200 to 800 apart.
All inputs are finite; a program needn't handle non-finite values.
Results may differ from the reference program's by a relative error of at most 0.00045.
Values sent between devices are 32-bit elements; how exact they have to be, the bound alone decides.
A program may use at most 64 MiB of HBM per device.

```python
import math
import jax
import jax.numpy as jnp
import numpy as np
from jax import lax

NODE = 512
STATE = 256
BUS = 256
CAP = 2
RULES = 16
KNOTS = 8
FEED_DEV = 16
SCEN = 64
LATERAL_COUNT = 128
AREAS = 8
HORIZON_TICKS = 24


def draw_decay_rate(key, part):
    speed_seed, surge_seed, multiplier_seed = jax.random.split(jax.random.fold_in(key, 11), 3)
    lowest = math.log(0.3 / HORIZON_TICKS)
    highest = math.log(1.0 / 30.0)
    spread = jax.random.uniform(speed_seed, (LATERAL_COUNT, 1, STATE), jnp.float32)
    rates = jnp.exp(lowest + (highest - lowest) * spread)
    nominal_magnitude = jnp.exp(-rates)
    surge_size = jax.random.uniform(surge_seed, (LATERAL_COUNT, HORIZON_TICKS, 1), jnp.float32) < 3.0 / HORIZON_TICKS
    multiplier_number = jax.random.uniform(multiplier_seed, (LATERAL_COUNT, HORIZON_TICKS, 1), jnp.float32, 0.5, 0.8)
    return (nominal_magnitude * jnp.where(surge_size, multiplier_number, 1.0)).astype(jnp.float32)


def draw_rule_knots(key, part):
    spacing = jax.random.randint(jax.random.fold_in(key, 23), (RULES, KNOTS), 200, 801).astype(jnp.int32)
    totals = jnp.cumsum(spacing, axis=1).astype(jnp.int32)
    middle = KNOTS // 2
    return (totals - totals[:, middle:middle + 1]).astype(jnp.int32)


def touch_ends(array, rng, smallest, high):
    place = [jax.random.randint(jax.random.fold_in(rng, axis), (), 0, length) for axis, length in enumerate(array.shape)]
    main_axis = array.shape.index(max(array.shape))
    next_to = place[:main_axis] + [(place[main_axis] + 1) % array.shape[main_axis]] + place[main_axis + 1:]
    return array.at[tuple(place)].set(smallest).at[tuple(next_to)].set(high)


def block_levels(rng, dims, cuts, smallest, largest):
    factor_of = 1.0
    for position, parts in cuts:
        heights = jax.random.uniform(jax.random.fold_in(jax.random.fold_in(rng, 6), position), (parts,), jnp.float32, smallest / len(cuts), largest / len(cuts))
        factor_of = factor_of * jnp.repeat(jnp.exp(heights), dims[position] // parts).reshape((-1,) + (1,) * (len(dims) - 1 - position))
    return factor_of


def shared_out(stream_key, own, number, rows, amount, top, bound, skew):
    sequence = jax.random.permutation(stream_key, amount)
    packed, ordinary = shares(amount, rows * top, bound, skew, True), shares(amount, rows * top, bound, skew, False)
    places = jnp.arange(amount)

    def named(lengths, turn):
        used = int((lengths > 0).sum())
        fixed = max(1, used // 4)
        moved = fixed + (places - fixed + turn * (used - fixed)) % max(1, amount - fixed)
        return jnp.zeros((amount,), jnp.int32).at[sequence[jnp.where(places < fixed, places, moved)]].set(jnp.asarray(lengths, jnp.int32))

    lengths = jnp.where(number % 4 == 0, named(packed, number // 4), named(ordinary, number - number // 4 - 1))
    mixed = jax.random.permutation(jax.random.fold_in(own, 3), amount)
    donor, sink = mixed[0:amount // 2 * 2:2], mixed[1:amount // 2 * 2:2]
    room = jnp.minimum(lengths[donor] - 1, bound - lengths[sink]) // 2
    room = jnp.where((donor == sequence[0]) | (sink == sequence[0]) | (lengths[sink] == 0), 0, jnp.maximum(room, 0))
    moved = jax.random.randint(jax.random.fold_in(own, 4), (amount // 2,), 0, 1 << 20) % (room + 1)
    lengths = lengths.at[donor].add(-moved).at[sink].add(moved)
    items = jnp.searchsorted(jnp.cumsum(lengths), jnp.arange(rows * top), side="right").astype(jnp.int32)
    grid = items.reshape(top, rows).T
    grid = grid[jax.random.permutation(jax.random.fold_in(own, 1), rows)]
    turn = jax.random.randint(jax.random.fold_in(own, 2), (rows, 1), 0, top)
    return jnp.take_along_axis(grid, (jnp.arange(top)[None, :] + turn) % top, axis=1)


def shares(amount, total, reach, skew, full):
    weights = [(1 << 20) // math.isqrt(standing ** skew) + 1 for standing in range(1, amount + 1)]
    largest = reach if full else min(reach, max(-(-total // amount), total * weights[0] // sum(weights)))
    least = 1 if total - largest >= amount - 1 else 0
    given, rest = [largest] + [least] * (amount - 1), total - largest - least * (amount - 1)
    while rest > 0:
        movable = [i for i in range(1, amount) if given[i] < largest] or [i for i in range(1, amount) if given[i] < reach]
        whole, left = sum([weights[i] for i in movable]), rest
        for i in movable:
            addition = min(reach - given[i], max(1, left * weights[i] // whole), rest)
            given[i] = given[i] + addition
            rest = rest - addition
    return np.array(given)


def gaussian(rng, dims, scale, limit, cuts=(), kind=jnp.bfloat16):
    level = block_levels(rng, dims, cuts, -0.22, 0.18) if cuts else 1.0
    array = jax.random.normal(rng, dims, jnp.float32) * scale * level
    return jnp.minimum(jnp.maximum(array, -limit), limit).astype(kind)


def setup_inputs(seed: int = 0) -> dict:
    keys = jax.random.split(jax.random.key(seed), 12)
    node_load = gaussian(keys[0], (LATERAL_COUNT, SCEN, HORIZON_TICKS, NODE), 1.0, 6.0, ((0, 8), (2, 4)))
    drive_map = gaussian(keys[1], (LATERAL_COUNT, NODE, STATE), NODE ** -0.5, 0.25, ((0, 8),))
    decay_rate = draw_decay_rate(jax.random.fold_in(keys[11], 71), 0)
    counts = touch_ends(jax.random.randint(keys[3], (LATERAL_COUNT,), STATE // 4, STATE + 1), jax.random.fold_in(keys[3], 1), STATE // 4, STATE).astype(jnp.int32)
    out_map = gaussian(keys[4], (LATERAL_COUNT, 2, STATE), STATE ** -0.5, 0.375, ((0, 8),), jnp.float32)
    area_of_keys = jax.random.split(jax.random.fold_in(keys[5], 1), LATERAL_COUNT // FEED_DEV)
    area_of_turns = jax.random.permutation(jax.random.fold_in(keys[5], 3), LATERAL_COUNT // FEED_DEV)
    area_of = jax.vmap(lambda own, number: shared_out(jax.random.fold_in(keys[5], 2), own, number, FEED_DEV, AREAS, 1, CAP, 2))(area_of_keys, area_of_turns).reshape((LATERAL_COUNT, 1))
    head_bus = touch_ends(jax.random.randint(keys[6], (LATERAL_COUNT,), 0, BUS), jax.random.fold_in(keys[6], 1), 0, BUS - 1).astype(jnp.int32)
    rule_of = touch_ends(jax.random.randint(keys[7], (LATERAL_COUNT,), 0, RULES), jax.random.fold_in(keys[7], 1), 0, RULES - 1).astype(jnp.int32)
    rule_knots = draw_rule_knots(jax.random.fold_in(keys[11], 71), 0)
    levels = touch_ends(jax.random.randint(keys[9], (RULES, KNOTS), -1000, 1001), jax.random.fold_in(keys[9], 1), -1000, 1000).astype(jnp.int32)
    sensitivity = gaussian(keys[10], (AREAS, 2, BUS, BUS), 0.1, 0.6, ((0, 8),), jnp.float32)
    return dict(node_load=node_load, drive_map=drive_map, decay_rate=decay_rate, counts=counts, out_map=out_map, area_of=area_of, head_bus=head_bus, rule_of=rule_of, rule_knots=rule_knots, levels=levels, sensitivity=sensitivity)


def setpoint_rule(volts, knot_volts, knot_levels):
    result = knot_levels[:, 0:1] + jnp.zeros_like(volts)
    for piece in range(knot_volts.shape[1] - 1):
        span_width = knot_volts[:, piece + 1:piece + 2] - knot_volts[:, piece:piece + 1]
        slope = (knot_levels[:, piece + 1:piece + 2] - knot_levels[:, piece:piece + 1]) / span_width
        result = result + slope * jnp.clip(volts - knot_volts[:, piece:piece + 1], 0.0, span_width)
    return result


def reference(node_load, drive_map, decay_rate, counts, out_map, area_of, head_bus, rule_of, rule_knots, levels, sensitivity):
    state_ids = jnp.arange(STATE, dtype=jnp.int32)

    def feeder_run(inputs):
        loads, mapping, retain, live_count, output_mapping = inputs
        live = (state_ids < live_count).astype(jnp.float32)
        drive = jnp.einsum('ctn,ns->cts', loads.astype(jnp.float32), mapping.astype(jnp.float32), precision=lax.Precision.HIGHEST) * live

        def advance(current, pair):
            keep, push = pair
            current = keep[None, :] * current + push
            return current, current

        _, history_record = lax.scan(advance, jnp.zeros((SCEN, STATE), jnp.float32), (retain, jnp.swapaxes(drive, 0, 1)))
        flow_value = jnp.einsum('dqp,up->udq', history_record, output_mapping, precision=lax.Precision.HIGHEST)
        return flow_value.reshape(2, HORIZON_TICKS * SCEN)

    head_flow = lax.map(feeder_run, (node_load, drive_map, decay_rate, counts, out_map))
    area_ids = area_of[:, 0]
    bus_hot = (head_bus[:, None] == jnp.arange(BUS, dtype=jnp.int32)[None, :]).astype(jnp.float32)

    def area_run(inputs):
        area_index, sens_block = inputs
        chosen = bus_hot * (area_ids == area_index).astype(jnp.float32)[:, None]
        bus_flow = jnp.einsum('fb,fkr->kbr', chosen, head_flow, precision=lax.Precision.HIGHEST)
        return jnp.einsum('kbe,ker->br', sens_block, bus_flow, precision=lax.Precision.HIGHEST)

    volt_shift = lax.map(area_run, (jnp.arange(AREAS, dtype=jnp.int32), sensitivity))
    volts = volt_shift[area_ids, head_bus]
    knot_volts = rule_knots.astype(jnp.float32)[rule_of] / 1000.0
    knot_levels = levels.astype(jnp.float32)[rule_of] / 1000.0
    settings = setpoint_rule(volts, knot_volts, knot_levels)
    return settings.reshape(LATERAL_COUNT, HORIZON_TICKS, SCEN)
```

```python
import functools

import jax
import jax.numpy as jnp
from jax import lax
from jax.experimental import pallas as pl
from jax.experimental.pallas import tpu as pltpu
from jax.sharding import PartitionSpec as P

HIGH = lax.Precision.HIGHEST
NT = (((1,), (1,)), ((), ()))
MESH = pl.DeviceIdType.MESH


def split(value):
    upper = value.astype(jnp.bfloat16).astype(jnp.float32)
    return upper, value - upper


def kernel(
    groups,
    turns,
    load_hbm,
    map_hbm,
    decay_ref,
    counts_ref,
    out_map_ref,
    area_ref,
    bus_ref,
    rule_ref,
    knots_ref,
    levels_ref,
    sens_hbm,
    out_ref,
    load_ref,
    map_ref,
    sens_ref,
    later_decay,
    pair_send,
    pair_recv,
    weight_ref,
    rule_vals,
    flow_ref,
    flow_send,
    flow_recv,
    volt_send,
    volt_recv,
    load_sem,
    map_sem,
    sens_sem,
    decay_sems,
    pair_sems,
    flow_sems,
    volt_sems,
):
    group, turn = lax.axis_index("feeder"), lax.axis_index("tm")
    per_dev, span, scen, nodes = load_ref.shape
    width = map_ref.shape[2]
    half = per_dev // 2
    couples = span // 2
    feeders = bus_ref.shape[1]
    buses = sens_ref.shape[1]
    rows = weight_ref.shape[1] // per_dev
    later_rows = (rows - 8) // 2
    piece = couples * 2 * half

    sens_copy = pltpu.make_async_copy(sens_hbm.at[0], sens_ref, sens_sem)
    sens_copy.start()

    def load_copies(f):
        return (
            pltpu.make_async_copy(load_hbm.at[f], load_ref.at[f], load_sem.at[f]),
            pltpu.make_async_copy(map_hbm.at[f], map_ref.at[f], map_sem.at[f]),
        )

    def start_loads(f, carry):
        for copy in load_copies(f):
            copy.start()
        return carry

    lax.fori_loop(0, per_dev, start_loads, 0)

    barrier = pltpu.get_barrier_semaphore()
    for step in range(1, turns):
        pl.semaphore_signal(
            barrier,
            inc=1,
            device_id=(group, lax.rem(turn + step, turns)),
            device_id_type=MESH,
        )
    for step in range(1, groups):
        pl.semaphore_signal(
            barrier,
            inc=1,
            device_id=(lax.rem(group + step, groups), turn),
            device_id_type=MESH,
        )
    pl.semaphore_wait(barrier, turns + groups - 2)

    def decay_copy(step):
        return pltpu.make_async_remote_copy(
            src_ref=decay_ref,
            dst_ref=later_decay.at[step - 1],
            send_sem=decay_sems.at[0, step - 1],
            recv_sem=decay_sems.at[1, step - 1],
            device_id=(group, turn - step),
            device_id_type=MESH,
        )

    for step in range(1, turns):

        @pl.when(turn >= step)
        def _():
            decay_copy(step).start()

    bus_ids = lax.broadcasted_iota(jnp.int32, (buses, feeders), 0)
    owned = (bus_ids == bus_ref[...]) & (area_ref[...] == group)
    hot = jnp.where(owned, 1.0, 0.0)
    hot_rows = hot.T
    sens_copy.wait()
    for k in range(2):
        picked = lax.dot_general(
            hot_rows, sens_ref[k], NT, precision=HIGH, preferred_element_type=jnp.float32
        )
        pairs = jnp.dot(picked, hot, precision=HIGH, preferred_element_type=jnp.float32)
        pair_send[:, k] = pairs.reshape(groups, per_dev, feeders)

    def pair_copy(step):
        target = lax.rem(group + step, groups)
        return pltpu.make_async_remote_copy(
            src_ref=pair_send.at[target],
            dst_ref=pair_recv.at[step - 1],
            send_sem=pair_sems.at[0, step - 1],
            recv_sem=pair_sems.at[1, step - 1],
            device_id=(target, turn),
            device_id_type=MESH,
        )

    for step in range(1, groups):
        pair_copy(step).start()

    rules = knots_ref.shape[1]
    rule_ids = lax.broadcasted_iota(jnp.int32, (rules, feeders), 0)
    rule_hot = jnp.where(rule_ids == rule_ref[...], 1.0, 0.0)
    table = jnp.concatenate(
        [knots_ref[...].astype(jnp.float32), levels_ref[...].astype(jnp.float32)], axis=0
    )
    chosen = jnp.dot(table, rule_hot, precision=HIGH, preferred_element_type=jnp.float32)
    rule_vals[...] = (chosen / 1000.0).T

    member = lax.broadcasted_iota(jnp.int32, (per_dev, width), 0)
    state_ids = lax.broadcasted_iota(jnp.int32, (per_dev, width), 1)
    limit = jnp.zeros((per_dev, width), jnp.int32)
    for f in range(per_dev):
        limit = jnp.where(member == f, counts_ref[f], limit)
    maps = [jnp.where(state_ids < limit, out_map_ref[:, k, :], 0.0) for k in range(2)]

    def put_rows(row, value):
        for lane in range(width // 128):
            weight_ref[lane, pl.ds(row, per_dev, stride=rows), :] = value[
                :, lane * 128 : (lane + 1) * 128
            ]

    for k in range(2):
        put_rows(k, maps[k])
    for step in range(1, turns):

        @pl.when(turn >= step)
        def _():
            decay_copy(step).wait_send()

        @pl.when(turn + step < turns)
        def _():
            decay_copy(step).wait_recv()

    product = jnp.ones((per_dev, width), jnp.float32)
    for step in range(turns - 1):
        for t in range(span):
            product = product * later_decay[step, t]
            for k in range(2):
                row = 8 + (t % 2) * later_rows + (step * couples + t // 2) * 2 + k
                put_rows(row, maps[k] * product)

    def feeder_flow(part, index, carry):
        f = part * half + index
        for copy in load_copies(f):
            copy.wait()
        drive = jnp.dot(
            load_ref[f].reshape(span * scen, nodes),
            map_ref[f],
            preferred_element_type=jnp.float32,
        )
        states = [drive[:scen]]
        for t in range(1, span):
            retain = decay_ref[t, pl.ds(f, 1), :]
            states.append(retain * states[-1] + drive[t * scen : (t + 1) * scen])
        upper, lower = split(jnp.concatenate(states, axis=0))
        both = jnp.concatenate([upper.astype(jnp.bfloat16), lower.astype(jnp.bfloat16)], axis=1)
        first = pl.multiple_of(f * rows, 8)
        weight = jnp.concatenate(
            [weight_ref[lane, pl.ds(first, rows), :] for lane in range(width // 128)], axis=1
        )
        w_upper, w_lower = split(weight)

        def doubled(start, stop):
            stacked = jnp.concatenate([w_upper[start:stop], w_lower[start:stop]], axis=0)
            stacked = stacked.astype(jnp.bfloat16)
            return jnp.concatenate([stacked, stacked], axis=1)

        local = lax.dot_general(doubled(0, 8), both, NT, preferred_element_type=jnp.float32)
        local = local[:8] + local[8:]
        for couple in range(couples):
            flow_ref[part, pl.ds(couple * 2 * half + index, 2, stride=half), :] = local[
                :2, couple * 2 * scen : (couple + 1) * 2 * scen
            ]
        if turns > 1:
            later = lax.dot_general(
                doubled(8, rows), both[(span - 1) * scen :], NT, preferred_element_type=jnp.float32
            )
            later = later[: 2 * later_rows] + later[2 * later_rows :]
            flow_send[part, pl.ds(index, later_rows, stride=half), :] = jnp.concatenate(
                [later[:later_rows], later[later_rows:]], axis=1
            )
        return carry

    def flow_copy(part, step):
        return pltpu.make_async_remote_copy(
            src_ref=flow_send.at[part, pl.ds((step - 1) * piece, piece)],
            dst_ref=flow_recv.at[part, step - 1],
            send_sem=flow_sems.at[0, part, step - 1],
            recv_sem=flow_sems.at[1, part, step - 1],
            device_id=(group, turn + step),
            device_id_type=MESH,
        )

    for part in range(2):
        lax.fori_loop(0, half, functools.partial(feeder_flow, part), 0)
        for step in range(1, turns):

            @pl.when(turn + step < turns)
            def _():
                flow_copy(part, step).start()

    effect = pair_send[group]
    for step in range(1, groups):
        pair_copy(step).wait()
        effect = effect + pair_recv[step - 1]
    effect = jnp.concatenate(
        [effect[k, part * half : (part + 1) * half] for part in range(2) for k in range(2)], axis=0
    ).T

    for part in range(2):
        for step in range(1, turns):

            @pl.when(turn >= step)
            def _():
                flow_copy(part, step).wait_recv()
                flow_ref[part] = flow_ref[part] + flow_recv[part, step - 1]

    for couple in range(couples):
        sources = jnp.concatenate(
            [flow_ref[part, couple * 2 * half : (couple + 1) * 2 * half] for part in range(2)],
            axis=0,
        )
        shift = jnp.dot(effect, sources, precision=HIGH, preferred_element_type=jnp.float32)
        volt_send[:, couple] = shift.reshape(groups, per_dev, 2 * scen)

    def volt_copy(step):
        target = lax.rem(group + step, groups)
        return pltpu.make_async_remote_copy(
            src_ref=volt_send.at[target],
            dst_ref=volt_recv.at[step - 1],
            send_sem=volt_sems.at[0, step - 1],
            recv_sem=volt_sems.at[1, step - 1],
            device_id=(target, turn),
            device_id_type=MESH,
        )

    for step in range(1, groups):
        volt_copy(step).start()

    mine = rule_vals[pl.ds(pl.multiple_of(group * per_dev, 8), per_dev), :]
    knot_count = knots_ref.shape[0]
    knots = [mine[:, i : i + 1] for i in range(knot_count)]
    levels = [mine[:, knot_count + i : knot_count + i + 1] for i in range(knot_count)]
    spans = [knots[i + 1] - knots[i] for i in range(knot_count - 1)]
    slopes = [(levels[i + 1] - levels[i]) / spans[i] for i in range(knot_count - 1)]
    volts = volt_send[group]
    for step in range(1, groups):
        volt_copy(step).wait_recv()
        volts = volts + volt_recv[step - 1]
    for couple in range(couples):
        value = volts[couple]
        result = levels[0] + jnp.zeros_like(value)
        for i in range(knot_count - 1):
            inside = jnp.minimum(jnp.maximum(value - knots[i], 0.0), spans[i])
            result = result + slopes[i] * inside
        out_ref[2 * couple] = result[:, :scen]
        out_ref[2 * couple + 1] = result[:, scen:]

    for step in range(1, groups):
        volt_copy(step).wait_send()
    for part in range(2):
        for step in range(1, turns):

            @pl.when(turn + step < turns)
            def _():
                flow_copy(part, step).wait_send()


def per_device(
    node_load,
    drive_map,
    decay_rate,
    counts,
    out_map,
    area_of,
    head_bus,
    rule_of,
    rule_knots,
    levels,
    sensitivity,
):
    groups, turns = lax.axis_size("feeder"), lax.axis_size("tm")
    per_dev, scen, span, nodes = node_load.shape
    width = drive_map.shape[2]
    feeders = head_bus.shape[0]
    buses = sensitivity.shape[2]
    half, couples = per_dev // 2, span // 2
    later_rows = -(-(turns - 1) * span // 8) * 8
    rows = 8 + 2 * later_rows
    piece = couples * 2 * half
    vmem = pl.BlockSpec(memory_space=pltpu.VMEM)
    hbm = pl.BlockSpec(memory_space=pltpu.HBM)
    smem = pl.BlockSpec(memory_space=pltpu.SMEM)
    f32 = jnp.float32
    dma = pltpu.SemaphoreType.DMA
    settings = pl.pallas_call(
        functools.partial(kernel, groups, turns),
        out_shape=jax.ShapeDtypeStruct((span, per_dev, scen), f32),
        in_specs=[hbm, hbm, vmem, smem, vmem, vmem, vmem, vmem, vmem, vmem, hbm],
        out_specs=vmem,
        scratch_shapes=[
            pltpu.VMEM((per_dev, span, scen, nodes), node_load.dtype),
            pltpu.VMEM((per_dev, nodes, width), drive_map.dtype),
            pltpu.VMEM((2, buses, buses), f32),
            pltpu.VMEM((turns - 1, span, per_dev, width), f32),
            pltpu.VMEM((groups, 2, per_dev, feeders), f32),
            pltpu.VMEM((groups - 1, 2, per_dev, feeders), f32),
            pltpu.VMEM((width // 128, per_dev * rows, 128), f32),
            pltpu.VMEM((feeders, 2 * rule_knots.shape[1]), f32),
            pltpu.VMEM((2, piece, 2 * scen), f32),
            pltpu.VMEM((2, later_rows * half, 2 * scen), f32),
            pltpu.VMEM((2, turns - 1, piece, 2 * scen), f32),
            pltpu.VMEM((groups, couples, per_dev, 2 * scen), f32),
            pltpu.VMEM((groups - 1, couples, per_dev, 2 * scen), f32),
            dma((per_dev,)),
            dma((per_dev,)),
            dma,
            dma((2, turns - 1)),
            dma((2, groups - 1)),
            dma((2, 2, turns - 1)),
            dma((2, groups - 1)),
        ],
        compiler_params=pltpu.CompilerParams(collective_id=0, has_side_effects=True),
    )(
        jnp.transpose(node_load, (0, 2, 1, 3)),
        drive_map,
        jnp.transpose(decay_rate, (1, 0, 2)),
        counts,
        out_map,
        area_of.reshape(1, feeders),
        head_bus.reshape(1, feeders),
        rule_of.reshape(1, feeders),
        rule_knots.T,
        levels.T,
        sensitivity,
    )
    return jnp.transpose(settings, (1, 0, 2))


def solution(mesh):
    return jax.shard_map(
        per_device,
        mesh=mesh,
        in_specs=(
            P("feeder", None, "tm", None),
            P("feeder", None, None),
            P("feeder", "tm", None),
            P("feeder"),
            P("feeder", None, None),
            P(),
            P(),
            P(),
            P(),
            P(),
            P("feeder", None, None, None),
        ),
        out_specs=P("feeder", "tm", None),
        check_vma=False,
    )
```

```python
import functools

import jax
import jax.numpy as jnp
from jax import lax
from jax.experimental import pallas as pl
from jax.experimental.pallas import tpu as pltpu
from jax.sharding import PartitionSpec as P

HIGH = lax.Precision.HIGHEST
NT = (((1,), (1,)), ((), ()))
MESH = pl.DeviceIdType.MESH
UNROLL = 4


def split(value):
    upper = value.astype(jnp.bfloat16).astype(jnp.float32)
    return upper, value - upper


def kernel(
    groups,
    turns,
    load_hbm,
    map_hbm,
    decay_ref,
    counts_ref,
    out_map_ref,
    area_ref,
    bus_ref,
    rule_ref,
    knots_ref,
    levels_ref,
    sens_hbm,
    out_ref,
    load_ref,
    map_ref,
    sens_ref,
    later_decay,
    pair_send,
    pair_recv,
    weight_ref,
    state_ref,
    column_ref,
    rule_vals,
    flow_ref,
    flow_send,
    flow_recv,
    volt_send,
    volt_recv,
    load_sem,
    map_sem,
    sens_sem,
    decay_sems,
    pair_sems,
    flow_sems,
    volt_sems,
):
    group, turn = lax.axis_index("feeder"), lax.axis_index("tm")
    per_dev, span, scen, nodes = load_ref.shape
    width = map_ref.shape[2]
    half = per_dev // 2
    couples = span // 2
    feeders = bus_ref.shape[1]
    buses = sens_ref.shape[1]
    rows = weight_ref.shape[1] // per_dev
    later_rows = rows // 2
    piece = couples * 2 * half

    sens_copy = pltpu.make_async_copy(sens_hbm.at[0], sens_ref, sens_sem)
    sens_copy.start()

    def load_copies(f):
        return (
            pltpu.make_async_copy(load_hbm.at[f], load_ref.at[f], load_sem.at[f]),
            pltpu.make_async_copy(map_hbm.at[f], map_ref.at[f], map_sem.at[f]),
        )

    def start_loads(f, carry):
        for copy in load_copies(f):
            copy.start()
        return carry

    lax.fori_loop(0, per_dev, start_loads, 0)

    barrier = pltpu.get_barrier_semaphore()
    for step in range(1, turns):
        pl.semaphore_signal(
            barrier,
            inc=1,
            device_id=(group, lax.rem(turn + step, turns)),
            device_id_type=MESH,
        )
    for step in range(1, groups):
        pl.semaphore_signal(
            barrier,
            inc=1,
            device_id=(lax.rem(group + step, groups), turn),
            device_id_type=MESH,
        )

    def decay_copy(step):
        return pltpu.make_async_remote_copy(
            src_ref=decay_ref,
            dst_ref=later_decay.at[step - 1],
            send_sem=decay_sems.at[0, step - 1],
            recv_sem=decay_sems.at[1, step - 1],
            device_id=(group, turn - step),
            device_id_type=MESH,
        )

    bus_ids = lax.broadcasted_iota(jnp.int32, (buses, feeders), 0)
    owned = (bus_ids == bus_ref[...]) & (area_ref[...] == group)
    hot = jnp.where(owned, 1.0, 0.0)
    hot_rows = hot.T
    sens_copy.wait()
    for k in range(2):
        picked = lax.dot_general(
            hot_rows, sens_ref[k], NT, precision=HIGH, preferred_element_type=jnp.float32
        )
        pairs = jnp.dot(picked, hot, precision=HIGH, preferred_element_type=jnp.float32)
        pair_send[:, k] = pairs.reshape(groups, per_dev, feeders)

    pl.semaphore_wait(barrier, turns + groups - 2)

    for step in range(1, turns):

        @pl.when(turn >= step)
        def _():
            decay_copy(step).start()

    def pair_copy(step):
        target = lax.rem(group + step, groups)
        return pltpu.make_async_remote_copy(
            src_ref=pair_send.at[target],
            dst_ref=pair_recv.at[step - 1],
            send_sem=pair_sems.at[0, step - 1],
            recv_sem=pair_sems.at[1, step - 1],
            device_id=(target, turn),
            device_id_type=MESH,
        )

    for step in range(1, groups):
        pair_copy(step).start()

    rules = knots_ref.shape[1]
    rule_ids = lax.broadcasted_iota(jnp.int32, (rules, feeders), 0)
    rule_hot = jnp.where(rule_ids == rule_ref[...], 1.0, 0.0)
    table = jnp.concatenate(
        [knots_ref[...].astype(jnp.float32), levels_ref[...].astype(jnp.float32)], axis=0
    )
    chosen = jnp.dot(table, rule_hot, precision=HIGH, preferred_element_type=jnp.float32)
    rule_vals[...] = (chosen / 1000.0).T

    member = lax.broadcasted_iota(jnp.int32, (per_dev, width), 0)
    state_ids = lax.broadcasted_iota(jnp.int32, (per_dev, width), 1)
    limit = jnp.zeros((per_dev, width), jnp.int32)
    for f in range(per_dev):
        limit = jnp.where(member == f, counts_ref[f], limit)
    maps = [jnp.where(state_ids < limit, out_map_ref[:, k, :], 0.0) for k in range(2)]

    def put_rows(row, value):
        for lane in range(width // 128):
            weight_ref[lane, pl.ds(row, per_dev, stride=rows), :] = value[
                :, lane * 128 : (lane + 1) * 128
            ]

    parts = [split(m) for m in maps]
    columns = [p[0] for p in parts] + [p[1] for p in parts]
    blank = jnp.zeros((128 - 4 * per_dev, width), jnp.float32)
    columns = jnp.concatenate(columns + [blank], axis=0).T.astype(jnp.bfloat16)
    lane_ids = lax.rem(lax.broadcasted_iota(jnp.int32, (1, 128), 1), per_dev)
    for f in range(per_dev):
        own = columns * jnp.where(lane_ids == f, 1.0, 0.0).astype(jnp.bfloat16)
        for copy in range(2):
            first = (2 * f + copy) * width
            column_ref[first : first + width] = own
    def feeder_states(f, carry):
        for copy in load_copies(f):
            copy.wait()
        drive = jnp.dot(
            load_ref[f].reshape(span * scen, nodes),
            map_ref[f],
            preferred_element_type=jnp.float32,
        )
        states = [drive[:scen]]
        for t in range(1, span):
            retain = decay_ref[t, pl.ds(f, 1), :]
            states.append(retain * states[-1] + drive[t * scen : (t + 1) * scen])
        upper, lower = split(jnp.concatenate(states, axis=0))
        first = pl.multiple_of(2 * f * width, 128)
        state_ref[:, pl.ds(first, width)] = upper.astype(jnp.bfloat16)
        state_ref[:, pl.ds(first + width, width)] = lower.astype(jnp.bfloat16)
        return carry

    def later_flow(part, index, carry):
        f = part * half + index
        first = pl.multiple_of(f * rows, 8)
        weight = jnp.concatenate(
            [weight_ref[lane, pl.ds(first, rows), :] for lane in range(width // 128)], axis=1
        )
        stacked = jnp.concatenate(split(weight), axis=0).astype(jnp.bfloat16)
        stacked = jnp.concatenate([stacked, stacked], axis=1)
        end = state_ref[(span - 1) * scen :, pl.ds(pl.multiple_of(2 * f * width, 128), 2 * width)]
        later = lax.dot_general(stacked, end, NT, preferred_element_type=jnp.float32)
        later = later[:rows] + later[rows:]
        flow_send[part, pl.ds(index, later_rows, stride=half), :] = jnp.concatenate(
            [later[:later_rows], later[later_rows:]], axis=1
        )
        return carry

    def flow_copy(part, step):
        return pltpu.make_async_remote_copy(
            src_ref=flow_send.at[part, pl.ds((step - 1) * piece, piece)],
            dst_ref=flow_recv.at[part, step - 1],
            send_sem=flow_sems.at[0, part, step - 1],
            recv_sem=flow_sems.at[1, part, step - 1],
            device_id=(group, turn + step),
            device_id_type=MESH,
        )

    lax.fori_loop(0, per_dev, feeder_states, 0, unroll=UNROLL)
    for step in range(1, turns):

        @pl.when(turn >= step)
        def _():
            decay_copy(step).wait_send()

        @pl.when(turn + step < turns)
        def _():
            decay_copy(step).wait_recv()

    product = jnp.ones((per_dev, width), jnp.float32)
    for step in range(turns - 1):
        for t in range(span):
            product = product * later_decay[step, t]
            for k in range(2):
                row = (t % 2) * later_rows + (step * couples + t // 2) * 2 + k
                put_rows(row, maps[k] * product)

    for part in range(2):
        if turns > 1:
            lax.fori_loop(0, half, functools.partial(later_flow, part), 0, unroll=UNROLL)
        for step in range(1, turns):

            @pl.when(turn + step < turns)
            def _():
                flow_copy(part, step).start()

    local = jnp.dot(state_ref[...], column_ref[...], preferred_element_type=jnp.float32).T
    local = local[: 2 * per_dev] + local[2 * per_dev : 4 * per_dev]
    flow_ref[...] = jnp.zeros_like(flow_ref)

    effect = pair_send[group]
    for step in range(1, groups):
        pair_copy(step).wait()
        effect = effect + pair_recv[step - 1]
    effect = jnp.concatenate(
        [effect[k, part * half : (part + 1) * half] for k in range(2) for part in range(2)], axis=0
    ).T

    for part in range(2):
        for step in range(1, turns):

            @pl.when(turn >= step)
            def _():
                flow_copy(part, step).wait_recv()
                flow_ref[part] = flow_ref[part] + flow_recv[part, step - 1]

    for couple in range(couples):
        arrived = [
            flow_ref[part, (couple * 2 + k) * half : (couple * 2 + k + 1) * half]
            for k in range(2)
            for part in range(2)
        ]
        sources = local[:, couple * 2 * scen : (couple + 1) * 2 * scen]
        sources = sources + jnp.concatenate(arrived, axis=0)
        shift = jnp.dot(effect, sources, precision=HIGH, preferred_element_type=jnp.float32)
        volt_send[:, couple] = shift.reshape(groups, per_dev, 2 * scen)

    def volt_copy(step):
        target = lax.rem(group + step, groups)
        return pltpu.make_async_remote_copy(
            src_ref=volt_send.at[target],
            dst_ref=volt_recv.at[step - 1],
            send_sem=volt_sems.at[0, step - 1],
            recv_sem=volt_sems.at[1, step - 1],
            device_id=(target, turn),
            device_id_type=MESH,
        )

    for step in range(1, groups):
        volt_copy(step).start()

    mine = rule_vals[pl.ds(pl.multiple_of(group * per_dev, 8), per_dev), :]
    knot_count = knots_ref.shape[0]
    knots = [mine[:, i : i + 1] for i in range(knot_count)]
    levels = [mine[:, knot_count + i : knot_count + i + 1] for i in range(knot_count)]
    spans = [knots[i + 1] - knots[i] for i in range(knot_count - 1)]
    slopes = [(levels[i + 1] - levels[i]) / spans[i] for i in range(knot_count - 1)]
    volts = volt_send[group]
    for step in range(1, groups):
        volt_copy(step).wait_recv()
        volts = volts + volt_recv[step - 1]
    for couple in range(couples):
        value = volts[couple]
        result = levels[0] + jnp.zeros_like(value)
        for i in range(knot_count - 1):
            inside = jnp.minimum(jnp.maximum(value - knots[i], 0.0), spans[i])
            result = result + slopes[i] * inside
        out_ref[2 * couple] = result[:, :scen]
        out_ref[2 * couple + 1] = result[:, scen:]

    for step in range(1, groups):
        volt_copy(step).wait_send()
    for part in range(2):
        for step in range(1, turns):

            @pl.when(turn + step < turns)
            def _():
                flow_copy(part, step).wait_send()


def per_device(
    node_load,
    drive_map,
    decay_rate,
    counts,
    out_map,
    area_of,
    head_bus,
    rule_of,
    rule_knots,
    levels,
    sensitivity,
):
    groups, turns = lax.axis_size("feeder"), lax.axis_size("tm")
    per_dev, scen, span, nodes = node_load.shape
    width = drive_map.shape[2]
    feeders = head_bus.shape[0]
    buses = sensitivity.shape[2]
    half, couples = per_dev // 2, span // 2
    later_rows = -(-(turns - 1) * span // 8) * 8
    rows = max(2 * later_rows, 8)
    piece = couples * 2 * half
    vmem = pl.BlockSpec(memory_space=pltpu.VMEM)
    hbm = pl.BlockSpec(memory_space=pltpu.HBM)
    smem = pl.BlockSpec(memory_space=pltpu.SMEM)
    f32 = jnp.float32
    dma = pltpu.SemaphoreType.DMA
    settings = pl.pallas_call(
        functools.partial(kernel, groups, turns),
        out_shape=jax.ShapeDtypeStruct((span, per_dev, scen), f32),
        in_specs=[hbm, hbm, vmem, smem, vmem, vmem, vmem, vmem, vmem, vmem, hbm],
        out_specs=vmem,
        scratch_shapes=[
            pltpu.VMEM((per_dev, span, scen, nodes), node_load.dtype),
            pltpu.VMEM((per_dev, nodes, width), drive_map.dtype),
            pltpu.VMEM((2, buses, buses), f32),
            pltpu.VMEM((turns - 1, span, per_dev, width), f32),
            pltpu.VMEM((groups, 2, per_dev, feeders), f32),
            pltpu.VMEM((groups - 1, 2, per_dev, feeders), f32),
            pltpu.VMEM((width // 128, per_dev * rows, 128), f32),
            pltpu.VMEM((span * scen, per_dev * 2 * width), jnp.bfloat16),
            pltpu.VMEM((per_dev * 2 * width, 128), jnp.bfloat16),
            pltpu.VMEM((feeders, 2 * rule_knots.shape[1]), f32),
            pltpu.VMEM((2, piece, 2 * scen), f32),
            pltpu.VMEM((2, later_rows * half, 2 * scen), f32),
            pltpu.VMEM((2, turns - 1, piece, 2 * scen), f32),
            pltpu.VMEM((groups, couples, per_dev, 2 * scen), f32),
            pltpu.VMEM((groups - 1, couples, per_dev, 2 * scen), f32),
            dma((per_dev,)),
            dma((per_dev,)),
            dma,
            dma((2, turns - 1)),
            dma((2, groups - 1)),
            dma((2, 2, turns - 1)),
            dma((2, groups - 1)),
        ],
        compiler_params=pltpu.CompilerParams(collective_id=0, has_side_effects=True),
    )(
        jnp.transpose(node_load, (0, 2, 1, 3)),
        drive_map,
        jnp.transpose(decay_rate, (1, 0, 2)),
        counts,
        out_map,
        area_of.reshape(1, feeders),
        head_bus.reshape(1, feeders),
        rule_of.reshape(1, feeders),
        rule_knots.T,
        levels.T,
        sensitivity,
    )
    return jnp.transpose(settings, (1, 0, 2))


def solution(mesh):
    return jax.shard_map(
        per_device,
        mesh=mesh,
        in_specs=(
            P("feeder", None, "tm", None),
            P("feeder", None, None),
            P("feeder", "tm", None),
            P("feeder"),
            P("feeder", None, None),
            P(),
            P(),
            P(),
            P(),
            P(),
            P("feeder", None, None, None),
        ),
        out_specs=P("feeder", "tm", None),
        check_vma=False,
    )
```

```python
import functools

import jax
import jax.numpy as jnp
from jax import lax
from jax.experimental import pallas as pl
from jax.experimental.pallas import tpu as pltpu
from jax.sharding import PartitionSpec as P

HIGH = lax.Precision.HIGHEST
NT = (((1,), (1,)), ((), ()))
MESH = pl.DeviceIdType.MESH
UNROLL = 8


def split(value):
    upper = value.astype(jnp.bfloat16).astype(jnp.float32)
    return upper, value - upper


def kernel(
    groups,
    turns,
    load_hbm,
    map_hbm,
    decay_ref,
    counts_ref,
    out_map_ref,
    area_ref,
    bus_ref,
    rule_ref,
    knots_ref,
    levels_ref,
    sens_hbm,
    out_ref,
    load_ref,
    map_ref,
    sens_ref,
    later_decay,
    pair_send,
    pair_recv,
    weight_ref,
    state_ref,
    column_ref,
    rule_vals,
    flow_ref,
    flow_send,
    flow_recv,
    volt_send,
    volt_recv,
    load_sem,
    map_sem,
    sens_sem,
    decay_sems,
    pair_sems,
    flow_sems,
    volt_sems,
):
    group, turn = lax.axis_index("feeder"), lax.axis_index("tm")
    per_dev, span, scen, nodes = load_ref.shape
    width = map_ref.shape[2]
    half = per_dev // 2
    couples = span // 2
    feeders = bus_ref.shape[1]
    buses = sens_ref.shape[1]
    rows = weight_ref.shape[1] // per_dev
    later_rows = rows // 2
    piece = couples * 2 * half

    sens_copy = pltpu.make_async_copy(sens_hbm.at[0], sens_ref, sens_sem)
    sens_copy.start()

    def load_copies(f):
        return (
            pltpu.make_async_copy(load_hbm.at[f], load_ref.at[f], load_sem.at[f]),
            pltpu.make_async_copy(map_hbm.at[f], map_ref.at[f], map_sem.at[f]),
        )

    def start_loads(f, carry):
        for copy in load_copies(f):
            copy.start()
        return carry

    lax.fori_loop(0, per_dev, start_loads, 0)

    barrier = pltpu.get_barrier_semaphore()
    for step in range(1, turns):
        pl.semaphore_signal(
            barrier,
            inc=1,
            device_id=(group, lax.rem(turn + step, turns)),
            device_id_type=MESH,
        )
    for step in range(1, groups):
        pl.semaphore_signal(
            barrier,
            inc=1,
            device_id=(lax.rem(group + step, groups), turn),
            device_id_type=MESH,
        )

    def decay_copy(step):
        return pltpu.make_async_remote_copy(
            src_ref=decay_ref,
            dst_ref=later_decay.at[step - 1],
            send_sem=decay_sems.at[0, step - 1],
            recv_sem=decay_sems.at[1, step - 1],
            device_id=(group, turn - step),
            device_id_type=MESH,
        )

    bus_ids = lax.broadcasted_iota(jnp.int32, (buses, feeders), 0)
    owned = (bus_ids == bus_ref[...]) & (area_ref[...] == group)
    hot = jnp.where(owned, 1.0, 0.0)
    hot_rows = hot.T.astype(jnp.bfloat16)
    hot = hot.astype(jnp.bfloat16)
    sens_copy.wait()
    for k in range(2):
        picked = sum(
            lax.dot_general(
                hot_rows, term.astype(jnp.bfloat16), NT, preferred_element_type=jnp.float32
            )
            for term in split(sens_ref[k])
        )
        pairs = sum(
            jnp.dot(term.astype(jnp.bfloat16), hot, preferred_element_type=jnp.float32)
            for term in split(picked)
        )
        pair_send[:, k] = pairs.reshape(groups, per_dev, feeders)

    pl.semaphore_wait(barrier, turns + groups - 2)

    for step in range(1, turns):

        @pl.when(turn >= step)
        def _():
            decay_copy(step).start()

    def pair_copy(step):
        target = lax.rem(group + step, groups)
        return pltpu.make_async_remote_copy(
            src_ref=pair_send.at[target],
            dst_ref=pair_recv.at[step - 1],
            send_sem=pair_sems.at[0, step - 1],
            recv_sem=pair_sems.at[1, step - 1],
            device_id=(target, turn),
            device_id_type=MESH,
        )

    for step in range(1, groups):
        pair_copy(step).start()

    rules = knots_ref.shape[1]
    rule_ids = lax.broadcasted_iota(jnp.int32, (rules, feeders), 0)
    rule_hot = jnp.where(rule_ids == rule_ref[...], 1.0, 0.0)
    table = jnp.concatenate(
        [knots_ref[...].astype(jnp.float32), levels_ref[...].astype(jnp.float32)], axis=0
    )
    chosen = jnp.dot(table, rule_hot, precision=HIGH, preferred_element_type=jnp.float32)
    rule_vals[...] = (chosen / 1000.0).T

    member = lax.broadcasted_iota(jnp.int32, (per_dev, width), 0)
    state_ids = lax.broadcasted_iota(jnp.int32, (per_dev, width), 1)
    limit = jnp.zeros((per_dev, width), jnp.int32)
    for f in range(per_dev):
        limit = jnp.where(member == f, counts_ref[f], limit)
    maps = [jnp.where(state_ids < limit, out_map_ref[:, k, :], 0.0) for k in range(2)]

    def put_rows(row, value):
        for lane in range(width // 128):
            weight_ref[lane, pl.ds(row, per_dev, stride=rows), :] = value[
                :, lane * 128 : (lane + 1) * 128
            ]

    parts = [split(m) for m in maps]
    columns = [p[0] for p in parts] + [p[1] for p in parts]
    blank = jnp.zeros((128 - 4 * per_dev, width), jnp.float32)
    columns = jnp.concatenate(columns + [blank], axis=0).T.astype(jnp.bfloat16)
    lane_ids = lax.rem(lax.broadcasted_iota(jnp.int32, (1, 128), 1), per_dev)
    for f in range(per_dev):
        own = columns * jnp.where(lane_ids == f, 1.0, 0.0).astype(jnp.bfloat16)
        for copy in range(2):
            first = (2 * f + copy) * width
            column_ref[first : first + width] = own
    def feeder_states(f, carry):
        for copy in load_copies(f):
            copy.wait()
        drive = jnp.dot(
            load_ref[f].reshape(span * scen, nodes),
            map_ref[f],
            preferred_element_type=jnp.float32,
        )
        states = [drive[:scen]]
        for t in range(1, span):
            retain = decay_ref[t, pl.ds(f, 1), :]
            states.append(retain * states[-1] + drive[t * scen : (t + 1) * scen])
        upper, lower = split(jnp.concatenate(states, axis=0))
        first = pl.multiple_of(2 * f * width, 128)
        state_ref[:, pl.ds(first, width)] = upper.astype(jnp.bfloat16)
        state_ref[:, pl.ds(first + width, width)] = lower.astype(jnp.bfloat16)
        return carry

    def later_flow(part, index, carry):
        f = part * half + index
        first = pl.multiple_of(f * rows, 8)
        weight = jnp.concatenate(
            [weight_ref[lane, pl.ds(first, rows), :] for lane in range(width // 128)], axis=1
        )
        stacked = jnp.concatenate(split(weight), axis=0).astype(jnp.bfloat16)
        stacked = jnp.concatenate([stacked, stacked], axis=1)
        end = state_ref[(span - 1) * scen :, pl.ds(pl.multiple_of(2 * f * width, 128), 2 * width)]
        later = lax.dot_general(stacked, end, NT, preferred_element_type=jnp.float32)
        later = later[:rows] + later[rows:]
        flow_send[part, pl.ds(index, later_rows, stride=half), :] = jnp.concatenate(
            [later[:later_rows], later[later_rows:]], axis=1
        )
        return carry

    def flow_copy(part, step):
        return pltpu.make_async_remote_copy(
            src_ref=flow_send.at[part, pl.ds((step - 1) * piece, piece)],
            dst_ref=flow_recv.at[part, step - 1],
            send_sem=flow_sems.at[0, part, step - 1],
            recv_sem=flow_sems.at[1, part, step - 1],
            device_id=(group, turn + step),
            device_id_type=MESH,
        )

    lax.fori_loop(0, per_dev, feeder_states, 0, unroll=UNROLL)
    for step in range(1, turns):

        @pl.when(turn >= step)
        def _():
            decay_copy(step).wait_send()

        @pl.when(turn + step < turns)
        def _():
            decay_copy(step).wait_recv()

    product = jnp.ones((per_dev, width), jnp.float32)
    for step in range(turns - 1):
        for t in range(span):
            product = product * later_decay[step, t]
            for k in range(2):
                row = (t % 2) * later_rows + (step * couples + t // 2) * 2 + k
                put_rows(row, maps[k] * product)

    for part in range(2):
        if turns > 1:
            lax.fori_loop(0, half, functools.partial(later_flow, part), 0, unroll=UNROLL)
        for step in range(1, turns):

            @pl.when(turn + step < turns)
            def _():
                flow_copy(part, step).start()

    local = jnp.dot(state_ref[...], column_ref[...], preferred_element_type=jnp.float32).T
    local = local[: 2 * per_dev] + local[2 * per_dev : 4 * per_dev]
    flow_ref[...] = jnp.zeros_like(flow_ref)

    effect = pair_send[group]
    for step in range(1, groups):
        pair_copy(step).wait()
        effect = effect + pair_recv[step - 1]
    effect = jnp.concatenate(
        [effect[k, part * half : (part + 1) * half] for k in range(2) for part in range(2)], axis=0
    ).T
    upper, lower = split(effect)
    effect = jnp.concatenate([upper, upper, lower], axis=1).astype(jnp.bfloat16)

    for part in range(2):
        for step in range(1, turns):

            @pl.when(turn >= step)
            def _():
                flow_copy(part, step).wait_recv()
                flow_ref[part] = flow_ref[part] + flow_recv[part, step - 1]

    for couple in range(couples):
        arrived = [
            flow_ref[part, (couple * 2 + k) * half : (couple * 2 + k + 1) * half]
            for k in range(2)
            for part in range(2)
        ]
        sources = local[:, couple * 2 * scen : (couple + 1) * 2 * scen]
        sources = sources + jnp.concatenate(arrived, axis=0)
        upper, lower = split(sources)
        sources = jnp.concatenate([upper, lower, upper], axis=0).astype(jnp.bfloat16)
        shift = jnp.dot(effect, sources, preferred_element_type=jnp.float32)
        volt_send[:, couple] = shift.reshape(groups, per_dev, 2 * scen)

    def volt_copy(step):
        target = lax.rem(group + step, groups)
        return pltpu.make_async_remote_copy(
            src_ref=volt_send.at[target],
            dst_ref=volt_recv.at[step - 1],
            send_sem=volt_sems.at[0, step - 1],
            recv_sem=volt_sems.at[1, step - 1],
            device_id=(target, turn),
            device_id_type=MESH,
        )

    for step in range(1, groups):
        volt_copy(step).start()

    mine = rule_vals[pl.ds(pl.multiple_of(group * per_dev, 8), per_dev), :]
    knot_count = knots_ref.shape[0]
    knots = [mine[:, i : i + 1] for i in range(knot_count)]
    levels = [mine[:, knot_count + i : knot_count + i + 1] for i in range(knot_count)]
    spans = [knots[i + 1] - knots[i] for i in range(knot_count - 1)]
    slopes = [(levels[i + 1] - levels[i]) / spans[i] for i in range(knot_count - 1)]
    volts = volt_send[group]
    for step in range(1, groups):
        volt_copy(step).wait_recv()
        volts = volts + volt_recv[step - 1]
    for couple in range(couples):
        value = volts[couple]
        result = levels[0] + jnp.zeros_like(value)
        for i in range(knot_count - 1):
            inside = jnp.minimum(jnp.maximum(value - knots[i], 0.0), spans[i])
            result = result + slopes[i] * inside
        out_ref[2 * couple] = result[:, :scen]
        out_ref[2 * couple + 1] = result[:, scen:]

    for step in range(1, groups):
        volt_copy(step).wait_send()
    for part in range(2):
        for step in range(1, turns):

            @pl.when(turn + step < turns)
            def _():
                flow_copy(part, step).wait_send()


def per_device(
    node_load,
    drive_map,
    decay_rate,
    counts,
    out_map,
    area_of,
    head_bus,
    rule_of,
    rule_knots,
    levels,
    sensitivity,
):
    groups, turns = lax.axis_size("feeder"), lax.axis_size("tm")
    per_dev, scen, span, nodes = node_load.shape
    width = drive_map.shape[2]
    feeders = head_bus.shape[0]
    buses = sensitivity.shape[2]
    half, couples = per_dev // 2, span // 2
    later_rows = -(-(turns - 1) * span // 8) * 8
    rows = max(2 * later_rows, 8)
    piece = couples * 2 * half
    vmem = pl.BlockSpec(memory_space=pltpu.VMEM)
    hbm = pl.BlockSpec(memory_space=pltpu.HBM)
    smem = pl.BlockSpec(memory_space=pltpu.SMEM)
    f32 = jnp.float32
    dma = pltpu.SemaphoreType.DMA
    settings = pl.pallas_call(
        functools.partial(kernel, groups, turns),
        out_shape=jax.ShapeDtypeStruct((span, per_dev, scen), f32),
        in_specs=[hbm, hbm, vmem, smem, vmem, vmem, vmem, vmem, vmem, vmem, hbm],
        out_specs=vmem,
        scratch_shapes=[
            pltpu.VMEM((per_dev, span, scen, nodes), node_load.dtype),
            pltpu.VMEM((per_dev, nodes, width), drive_map.dtype),
            pltpu.VMEM((2, buses, buses), f32),
            pltpu.VMEM((turns - 1, span, per_dev, width), f32),
            pltpu.VMEM((groups, 2, per_dev, feeders), f32),
            pltpu.VMEM((groups - 1, 2, per_dev, feeders), f32),
            pltpu.VMEM((width // 128, per_dev * rows, 128), f32),
            pltpu.VMEM((span * scen, per_dev * 2 * width), jnp.bfloat16),
            pltpu.VMEM((per_dev * 2 * width, 128), jnp.bfloat16),
            pltpu.VMEM((feeders, 2 * rule_knots.shape[1]), f32),
            pltpu.VMEM((2, piece, 2 * scen), f32),
            pltpu.VMEM((2, later_rows * half, 2 * scen), f32),
            pltpu.VMEM((2, turns - 1, piece, 2 * scen), f32),
            pltpu.VMEM((groups, couples, per_dev, 2 * scen), f32),
            pltpu.VMEM((groups - 1, couples, per_dev, 2 * scen), f32),
            dma((per_dev,)),
            dma((per_dev,)),
            dma,
            dma((2, turns - 1)),
            dma((2, groups - 1)),
            dma((2, 2, turns - 1)),
            dma((2, groups - 1)),
        ],
        compiler_params=pltpu.CompilerParams(collective_id=0, has_side_effects=True),
    )(
        jnp.transpose(node_load, (0, 2, 1, 3)),
        drive_map,
        jnp.transpose(decay_rate, (1, 0, 2)),
        counts,
        out_map,
        area_of.reshape(1, feeders),
        head_bus.reshape(1, feeders),
        rule_of.reshape(1, feeders),
        rule_knots.T,
        levels.T,
        sensitivity,
    )
    return jnp.transpose(settings, (1, 0, 2))


def solution(mesh):
    return jax.shard_map(
        per_device,
        mesh=mesh,
        in_specs=(
            P("feeder", None, "tm", None),
            P("feeder", None, None),
            P("feeder", "tm", None),
            P("feeder"),
            P("feeder", None, None),
            P(),
            P(),
            P(),
            P(),
            P(),
            P("feeder", None, None, None),
        ),
        out_specs=P("feeder", "tm", None),
        check_vma=False,
    )
```

```python
import functools

import jax
import jax.numpy as jnp
from jax import lax
from jax.experimental import pallas as pl
from jax.experimental.pallas import tpu as pltpu
from jax.sharding import PartitionSpec as P

HIGH = lax.Precision.HIGHEST
NT = (((1,), (1,)), ((), ()))
MESH = pl.DeviceIdType.MESH
UNROLL = 8


def split(value):
    upper = value.astype(jnp.bfloat16).astype(jnp.float32)
    return upper, value - upper


def kernel(
    groups,
    turns,
    load_hbm,
    map_hbm,
    decay_ref,
    counts_ref,
    out_map_ref,
    area_ref,
    bus_ref,
    rule_ref,
    knots_ref,
    levels_ref,
    sens_hbm,
    out_ref,
    load_ref,
    map_ref,
    sens_ref,
    later_decay,
    pair_send,
    pair_recv,
    weight_ref,
    state_ref,
    column_ref,
    rule_vals,
    flow_ref,
    flow_send,
    flow_recv,
    volt_send,
    volt_recv,
    load_sem,
    map_sem,
    sens_sem,
    decay_sems,
    pair_sems,
    flow_sems,
    volt_sems,
):
    group, turn = lax.axis_index("feeder"), lax.axis_index("tm")
    per_dev, span, scen, nodes = load_ref.shape
    width = map_ref.shape[2]
    half = per_dev // 2
    couples = span // 2
    feeders = bus_ref.shape[1]
    buses = sens_ref.shape[1]
    rows = weight_ref.shape[1] // per_dev
    later_rows = rows // 2
    piece = couples * 2 * half

    sens_copy = pltpu.make_async_copy(sens_hbm.at[0], sens_ref, sens_sem)
    sens_copy.start()

    def load_copies(f):
        return (
            pltpu.make_async_copy(load_hbm.at[f], load_ref.at[f], load_sem.at[f]),
            pltpu.make_async_copy(map_hbm.at[f], map_ref.at[f], map_sem.at[f]),
        )

    def start_loads(f, carry):
        for copy in load_copies(f):
            copy.start()
        return carry

    lax.fori_loop(0, per_dev, start_loads, 0)

    barrier = pltpu.get_barrier_semaphore()
    for step in range(1, turns):
        pl.semaphore_signal(
            barrier,
            inc=1,
            device_id=(group, lax.rem(turn + step, turns)),
            device_id_type=MESH,
        )
    for step in range(1, groups):
        pl.semaphore_signal(
            barrier,
            inc=1,
            device_id=(lax.rem(group + step, groups), turn),
            device_id_type=MESH,
        )

    def decay_copy(step):
        return pltpu.make_async_remote_copy(
            src_ref=decay_ref,
            dst_ref=later_decay.at[step - 1],
            send_sem=decay_sems.at[0, step - 1],
            recv_sem=decay_sems.at[1, step - 1],
            device_id=(group, turn - step),
            device_id_type=MESH,
        )

    bus_ids = lax.broadcasted_iota(jnp.int32, (buses, feeders), 0)
    owned = (bus_ids == bus_ref[...]) & (area_ref[...] == group)
    hot = jnp.where(owned, 1.0, 0.0)
    hot_rows = hot.T.astype(jnp.bfloat16)
    hot = hot.astype(jnp.bfloat16)
    sens_copy.wait()
    for k in range(2):
        picked = sum(
            lax.dot_general(
                hot_rows, term.astype(jnp.bfloat16), NT, preferred_element_type=jnp.float32
            )
            for term in split(sens_ref[k])
        )
        pairs = sum(
            jnp.dot(term.astype(jnp.bfloat16), hot, preferred_element_type=jnp.float32)
            for term in split(picked)
        )
        pair_send[:, k] = pairs.reshape(groups, per_dev, feeders)

    pl.semaphore_wait(barrier, turns + groups - 2)

    for step in range(1, turns):

        @pl.when(turn >= step)
        def _():
            decay_copy(step).start()

    def pair_copy(step):
        target = lax.rem(group + step, groups)
        return pltpu.make_async_remote_copy(
            src_ref=pair_send.at[target],
            dst_ref=pair_recv.at[step - 1],
            send_sem=pair_sems.at[0, step - 1],
            recv_sem=pair_sems.at[1, step - 1],
            device_id=(target, turn),
            device_id_type=MESH,
        )

    for step in range(1, groups):
        pair_copy(step).start()

    rules = knots_ref.shape[1]
    rule_ids = lax.broadcasted_iota(jnp.int32, (rules, feeders), 0)
    rule_hot = jnp.where(rule_ids == rule_ref[...], 1.0, 0.0)
    table = jnp.concatenate(
        [knots_ref[...].astype(jnp.float32), levels_ref[...].astype(jnp.float32)], axis=0
    )
    chosen = jnp.dot(table, rule_hot, precision=HIGH, preferred_element_type=jnp.float32)
    rule_vals[...] = (chosen / 1000.0).T

    member = lax.broadcasted_iota(jnp.int32, (per_dev, width), 0)
    state_ids = lax.broadcasted_iota(jnp.int32, (per_dev, width), 1)
    limit = jnp.zeros((per_dev, width), jnp.int32)
    for f in range(per_dev):
        limit = jnp.where(member == f, counts_ref[f], limit)
    maps = [jnp.where(state_ids < limit, out_map_ref[:, k, :], 0.0) for k in range(2)]

    def put_rows(row, value):
        for lane in range(width // 128):
            weight_ref[lane, pl.ds(row, per_dev, stride=rows), :] = value[
                :, lane * 128 : (lane + 1) * 128
            ]

    parts = [split(m) for m in maps]
    columns = [p[0] for p in parts] + [p[1] for p in parts]
    blank = jnp.zeros((128 - 4 * per_dev, width), jnp.float32)
    columns = jnp.concatenate(columns + [blank], axis=0).T.astype(jnp.bfloat16)
    lane_ids = lax.rem(lax.broadcasted_iota(jnp.int32, (1, 128), 1), per_dev)
    for f in range(per_dev):
        own = columns * jnp.where(lane_ids == f, 1.0, 0.0).astype(jnp.bfloat16)
        for copy in range(2):
            first = (2 * f + copy) * width
            column_ref[first : first + width] = own
    def feeder_states(f, carry):
        for copy in load_copies(f):
            copy.wait()
        drive = jnp.dot(
            load_ref[f].reshape(span * scen, nodes),
            map_ref[f],
            preferred_element_type=jnp.float32,
        )
        states = [drive[:scen]]
        for t in range(1, span):
            retain = decay_ref[t, pl.ds(f, 1), :]
            states.append(retain * states[-1] + drive[t * scen : (t + 1) * scen])
        upper, lower = split(jnp.concatenate(states, axis=0))
        first = pl.multiple_of(2 * f * width, 128)
        state_ref[:, pl.ds(first, width)] = upper.astype(jnp.bfloat16)
        state_ref[:, pl.ds(first + width, width)] = lower.astype(jnp.bfloat16)
        return carry

    def later_flow(part, index, carry):
        f = part * half + index
        first = pl.multiple_of(f * rows, 8)
        weight = jnp.concatenate(
            [weight_ref[lane, pl.ds(first, rows), :] for lane in range(width // 128)], axis=1
        )
        stacked = jnp.concatenate(split(weight), axis=0).astype(jnp.bfloat16)
        stacked = jnp.concatenate([stacked, stacked], axis=1)
        end = state_ref[(span - 1) * scen :, pl.ds(pl.multiple_of(2 * f * width, 128), 2 * width)]
        later = lax.dot_general(stacked, end, NT, preferred_element_type=jnp.float32)
        later = later[:rows] + later[rows:]
        flow_send[part, pl.ds(index, later_rows, stride=half), :] = jnp.concatenate(
            [later[:later_rows], later[later_rows:]], axis=1
        )
        return carry

    def flow_copy(part, step):
        return pltpu.make_async_remote_copy(
            src_ref=flow_send.at[part, pl.ds((step - 1) * piece, piece)],
            dst_ref=flow_recv.at[part, step - 1],
            send_sem=flow_sems.at[0, part, step - 1],
            recv_sem=flow_sems.at[1, part, step - 1],
            device_id=(group, turn + step),
            device_id_type=MESH,
        )

    lax.fori_loop(0, per_dev, feeder_states, 0, unroll=per_dev)
    for step in range(1, turns):

        @pl.when(turn >= step)
        def _():
            decay_copy(step).wait_send()

        @pl.when(turn + step < turns)
        def _():
            decay_copy(step).wait_recv()

    product = jnp.ones((per_dev, width), jnp.float32)
    for step in range(turns - 1):
        for t in range(span):
            product = product * later_decay[step, t]
            for k in range(2):
                row = (t % 2) * later_rows + (step * couples + t // 2) * 2 + k
                put_rows(row, maps[k] * product)

    for part in range(2):
        if turns > 1:
            lax.fori_loop(0, half, functools.partial(later_flow, part), 0, unroll=UNROLL)
        for step in range(1, turns):

            @pl.when(turn + step < turns)
            def _():
                flow_copy(part, step).start()

    local = jnp.dot(state_ref[...], column_ref[...], preferred_element_type=jnp.float32).T
    local = local[: 2 * per_dev] + local[2 * per_dev : 4 * per_dev]
    flow_ref[...] = jnp.zeros_like(flow_ref)

    effect = pair_send[group]
    for step in range(1, groups):
        pair_copy(step).wait()
        effect = effect + pair_recv[step - 1]
    effect = jnp.concatenate(
        [effect[k, part * half : (part + 1) * half] for k in range(2) for part in range(2)], axis=0
    ).T
    upper, lower = split(effect)
    effect = jnp.concatenate([upper, upper, lower], axis=1).astype(jnp.bfloat16)

    for part in range(2):
        for step in range(1, turns):

            @pl.when(turn >= step)
            def _():
                flow_copy(part, step).wait_recv()
                flow_ref[part] = flow_ref[part] + flow_recv[part, step - 1]

    for couple in range(couples):
        arrived = [
            flow_ref[part, (couple * 2 + k) * half : (couple * 2 + k + 1) * half]
            for k in range(2)
            for part in range(2)
        ]
        sources = local[:, couple * 2 * scen : (couple + 1) * 2 * scen]
        sources = sources + jnp.concatenate(arrived, axis=0)
        upper, lower = split(sources)
        sources = jnp.concatenate([upper, lower, upper], axis=0).astype(jnp.bfloat16)
        shift = jnp.dot(effect, sources, preferred_element_type=jnp.float32)
        volt_send[:, couple] = shift.reshape(groups, per_dev, 2 * scen)

    def volt_copy(step):
        target = lax.rem(group + step, groups)
        return pltpu.make_async_remote_copy(
            src_ref=volt_send.at[target],
            dst_ref=volt_recv.at[step - 1],
            send_sem=volt_sems.at[0, step - 1],
            recv_sem=volt_sems.at[1, step - 1],
            device_id=(target, turn),
            device_id_type=MESH,
        )

    for step in range(1, groups):
        volt_copy(step).start()

    mine = rule_vals[pl.ds(pl.multiple_of(group * per_dev, 8), per_dev), :]
    knot_count = knots_ref.shape[0]
    knots = [mine[:, i : i + 1] for i in range(knot_count)]
    levels = [mine[:, knot_count + i : knot_count + i + 1] for i in range(knot_count)]
    spans = [knots[i + 1] - knots[i] for i in range(knot_count - 1)]
    slopes = [(levels[i + 1] - levels[i]) / spans[i] for i in range(knot_count - 1)]
    volts = volt_send[group]
    for step in range(1, groups):
        volt_copy(step).wait_recv()
        volts = volts + volt_recv[step - 1]
    for couple in range(couples):
        value = volts[couple]
        result = levels[0] + jnp.zeros_like(value)
        for i in range(knot_count - 1):
            inside = jnp.minimum(jnp.maximum(value - knots[i], 0.0), spans[i])
            result = result + slopes[i] * inside
        out_ref[2 * couple] = result[:, :scen]
        out_ref[2 * couple + 1] = result[:, scen:]

    for step in range(1, groups):
        volt_copy(step).wait_send()
    for part in range(2):
        for step in range(1, turns):

            @pl.when(turn + step < turns)
            def _():
                flow_copy(part, step).wait_send()


def per_device(
    node_load,
    drive_map,
    decay_rate,
    counts,
    out_map,
    area_of,
    head_bus,
    rule_of,
    rule_knots,
    levels,
    sensitivity,
):
    groups, turns = lax.axis_size("feeder"), lax.axis_size("tm")
    per_dev, scen, span, nodes = node_load.shape
    width = drive_map.shape[2]
    feeders = head_bus.shape[0]
    buses = sensitivity.shape[2]
    half, couples = per_dev // 2, span // 2
    later_rows = -(-(turns - 1) * span // 8) * 8
    rows = max(2 * later_rows, 8)
    piece = couples * 2 * half
    vmem = pl.BlockSpec(memory_space=pltpu.VMEM)
    hbm = pl.BlockSpec(memory_space=pltpu.HBM)
    smem = pl.BlockSpec(memory_space=pltpu.SMEM)
    f32 = jnp.float32
    dma = pltpu.SemaphoreType.DMA
    settings = pl.pallas_call(
        functools.partial(kernel, groups, turns),
        out_shape=jax.ShapeDtypeStruct((span, per_dev, scen), f32),
        in_specs=[hbm, hbm, vmem, smem, vmem, vmem, vmem, vmem, vmem, vmem, hbm],
        out_specs=vmem,
        scratch_shapes=[
            pltpu.VMEM((per_dev, span, scen, nodes), node_load.dtype),
            pltpu.VMEM((per_dev, nodes, width), drive_map.dtype),
            pltpu.VMEM((2, buses, buses), f32),
            pltpu.VMEM((turns - 1, span, per_dev, width), f32),
            pltpu.VMEM((groups, 2, per_dev, feeders), f32),
            pltpu.VMEM((groups - 1, 2, per_dev, feeders), f32),
            pltpu.VMEM((width // 128, per_dev * rows, 128), f32),
            pltpu.VMEM((span * scen, per_dev * 2 * width), jnp.bfloat16),
            pltpu.VMEM((per_dev * 2 * width, 128), jnp.bfloat16),
            pltpu.VMEM((feeders, 2 * rule_knots.shape[1]), f32),
            pltpu.VMEM((2, piece, 2 * scen), f32),
            pltpu.VMEM((2, later_rows * half, 2 * scen), f32),
            pltpu.VMEM((2, turns - 1, piece, 2 * scen), f32),
            pltpu.VMEM((groups, couples, per_dev, 2 * scen), f32),
            pltpu.VMEM((groups - 1, couples, per_dev, 2 * scen), f32),
            dma((per_dev,)),
            dma((per_dev,)),
            dma,
            dma((2, turns - 1)),
            dma((2, groups - 1)),
            dma((2, 2, turns - 1)),
            dma((2, groups - 1)),
        ],
        compiler_params=pltpu.CompilerParams(collective_id=0, has_side_effects=True),
    )(
        jnp.transpose(node_load, (0, 2, 1, 3)),
        drive_map,
        jnp.transpose(decay_rate, (1, 0, 2)),
        counts,
        out_map,
        area_of.reshape(1, feeders),
        head_bus.reshape(1, feeders),
        rule_of.reshape(1, feeders),
        rule_knots.T,
        levels.T,
        sensitivity,
    )
    return jnp.transpose(settings, (1, 0, 2))


def solution(mesh):
    return jax.shard_map(
        per_device,
        mesh=mesh,
        in_specs=(
            P("feeder", None, "tm", None),
            P("feeder", None, None),
            P("feeder", "tm", None),
            P("feeder"),
            P("feeder", None, None),
            P(),
            P(),
            P(),
            P(),
            P(),
            P("feeder", None, None, None),
        ),
        out_specs=P("feeder", "tm", None),
        check_vma=False,
    )
```
